1024 devices in a mesh: context: 64 (over z, x), channel: 16 (over y, core).
Axes of the slice: x: 8, y: 8, z: 8, core: 2. Of those that a mesh axis runs over, the one named last changes fastest.
Arguments:
- first_stream: bfloat16 [16384, 8192], P('context', 'channel'), may hold values from -6 to 6
- value_stream: bfloat16 [16384, 8192], P('context', 'channel'), may hold values from -6 to 6
- short_gate: bfloat16 [16384, 8192], P('context', 'channel'), may hold values from -6 to 6
- out_gate: bfloat16 [16384, 8192], P('context', 'channel'), may hold values from -250 to 250
- mr_filter: float32 [128, 8192], P(None, 'channel'), may hold values from -0.5 to 0.5
- li_residue: float32 [16, 8192], P(None, 'channel'), may hold values from -1.5 to 1.5
- li_rate: float32 [16, 8192], P(None, 'channel'), may hold values from 1.8310548e-05 to 0.05
- li_skip: float32 [8192], P('channel'), may hold values from 0.5 to 1.5
- norm_gain: float32 [8192], P('channel'), may hold values from 0.5 to 1.5
Outputs:
- mixed: bfloat16 [16384, 8192], P('context', 'channel')
The draws below stay inside these ranges and needn't reach their ends.
All inputs are finite; a program needn't handle non-finite values.
Results may differ from the reference program's by a relative error of at most 0.0064.
Values may be sent and summed in bfloat16 or wider, within the bound.
No kernel may reach another device: no remote copies, remote signals or barrier semaphores. Data moves between devices by JAX's collectives and lax.ppermute only.
A program may use at most 32 MiB of HBM per device.

```python
import math
import jax
import jax.numpy as jnp
from jax import lax

D = 8192
TAPS = 128
POLES = 16
LENGTH = 16384
NFFT = 32768


def draw_out_gate(key, part):
    key_base = jax.random.fold_in(key, 11)
    key_col = jax.random.fold_in(key, 12)
    key_row = jax.random.fold_in(key, 13)
    columns = jnp.arange(D).astype(jnp.float32)
    col_scale = 10.0 ** (columns / D) * 2.0 ** jax.random.uniform(key_col, (D,), jnp.float32)
    row_scale = 10.0 ** jax.random.uniform(key_row, (LENGTH, 1), jnp.float32)
    base = jnp.clip(jax.random.normal(key_base, (LENGTH, D), jnp.float32), -5.0, 5.0)
    return (base * col_scale[None, :] * row_scale / 4.0).astype(jnp.bfloat16)


def block_scale(key, dims, shards, smallest, largest):
    def one(position, shards_of):
        steps = jax.random.uniform(jax.random.fold_in(jax.random.fold_in(key, 6), position), (shards_of,), jnp.float32, smallest / len(shards), largest / len(shards))
        return jnp.repeat(jnp.exp(steps), dims[position] // shards_of).reshape((-1,) + (1,) * (len(dims) - position - 1))

    level = one(*shards[0])
    for cut in shards[1:]:
        level = level * one(*cut)
    return level


def gaussian(key, extent, deviation, reach, split=(), kind=jnp.bfloat16):
    values = jax.random.normal(key, extent, jnp.float32) * deviation
    if len(split) > 0:
        values = block_scale(key, extent, split, -0.22, 0.18) * values
    return jnp.clip(values, min=-reach, max=reach).astype(kind)


def setup_inputs(seed: int = 0) -> dict:
    arg_keys = jax.random.split(jax.random.key(seed), 10)
    first_stream = gaussian(arg_keys[0], (LENGTH, D), 1.0, 6.0, ((0, 64), (1, 16)))
    value_stream = gaussian(arg_keys[1], (LENGTH, D), 1.0, 6.0, ((0, 64), (1, 16)))
    short_gate = gaussian(arg_keys[2], (LENGTH, D), 1.0, 6.0, ((0, 64), (1, 16)))
    out_gate = draw_out_gate(jax.random.fold_in(arg_keys[9], 71), 0)
    mr_filter = gaussian(arg_keys[4], (TAPS, D), TAPS ** -0.5, 0.5, ((1, 16),), jnp.float32)
    li_residue = gaussian(arg_keys[5], (POLES, D), 0.25, 1.5, ((1, 16),), jnp.float32)
    li_rate = jnp.clip(jnp.exp(math.log(0.05) - 7.912301 * jax.random.uniform(arg_keys[6], (POLES, D), jnp.float32) ** block_scale(arg_keys[6], (POLES, D), ((1, 16),), -0.2, 0.2)), 1.831054760259576e-05, 0.05)
    li_skip = jnp.clip(0.5 + 1.0 * jax.random.uniform(arg_keys[7], (D,), jnp.float32) ** block_scale(arg_keys[7], (D,), ((0, 16),), -0.2, 0.2), 0.5, 1.5)
    norm_gain = jnp.clip(1.0 + 0.1 * jax.random.normal(arg_keys[8], (D,), jnp.float32), 0.5, 1.5)
    return dict(first_stream=first_stream, value_stream=value_stream, short_gate=short_gate, out_gate=out_gate, mr_filter=mr_filter, li_residue=li_residue, li_rate=li_rate, li_skip=li_skip, norm_gain=norm_gain)


def column_block(array, index, width):
    return lax.dynamic_slice_in_dim(array, (index * width).astype(jnp.int32), width, array.ndim - 1)

def short_block(product, taps_block):
    signal = product.astype(jnp.float32)
    padded = jnp.concatenate([jnp.zeros((TAPS - 1, signal.shape[1]), jnp.float32), signal], 0)

    def add_tap(tap, total):
        start = (TAPS - 1 - tap).astype(jnp.int32)
        window = lax.dynamic_slice_in_dim(padded, start, LENGTH, 0)
        weight = lax.dynamic_slice_in_dim(taps_block, tap.astype(jnp.int32), 1, 0)
        return total + weight * window
    return lax.fori_loop(jnp.int32(0), jnp.int32(TAPS), add_tap, jnp.zeros((LENGTH, signal.shape[1]), jnp.float32))

def long_block(sequence, residue, rate):
    times = jnp.arange(LENGTH).astype(jnp.float32)
    impulse = jnp.zeros((LENGTH, sequence.shape[1]), jnp.float32)
    for index in range(POLES):
        impulse = impulse + residue[index][None, :] * jnp.sqrt(2.0 * rate[index][None, :]) * jnp.exp(-rate[index][None, :] * times[:, None])
    spectrum = jnp.fft.rfft(sequence.astype(jnp.float32), n=NFFT, axis=0) * jnp.fft.rfft(impulse, n=NFFT, axis=0)
    return jnp.fft.irfft(spectrum, n=NFFT, axis=0)[:LENGTH].astype(jnp.float32)

def reference(first_stream, value_stream, short_gate, out_gate, mr_filter, li_residue, li_rate, li_skip, norm_gain):
    width = 256
    blocks = D // width
    indices = jnp.arange(blocks).astype(jnp.int32)

    def first_pass(power_sum, index):
        first = column_block(first_stream, index, width).astype(jnp.float32)
        value = column_block(value_stream, index, width).astype(jnp.float32)
        product = (first * value).astype(jnp.bfloat16)
        short = short_block(product, column_block(mr_filter, index, width))
        mixed_short = (column_block(short_gate, index, width).astype(jnp.float32) * short).astype(jnp.bfloat16)
        long_conv = long_block(mixed_short, column_block(li_residue, index, width), column_block(li_rate, index, width))
        skip = column_block(li_skip, index, width)
        long_out = (long_conv + skip[None, :] * mixed_short.astype(jnp.float32)).astype(jnp.bfloat16)
        gated = column_block(out_gate, index, width).astype(jnp.float32) * long_out.astype(jnp.float32)
        return (power_sum + lax.optimization_barrier(jnp.sum(gated * gated, axis=1)), long_out)
    power_sum, long_blocks = lax.scan(first_pass, jnp.zeros((LENGTH,), jnp.float32), indices)
    scale = lax.rsqrt(power_sum / D + 1e-06)

    def second_pass(carry, pack):
        index, long_out = pack
        gated = column_block(out_gate, index, width).astype(jnp.float32) * long_out.astype(jnp.float32)
        gains = column_block(norm_gain, index, width)
        return (carry, (gated * scale[:, None] * gains[None, :]).astype(jnp.bfloat16))
    _, out_blocks = lax.scan(second_pass, jnp.zeros((), jnp.float32), (indices, long_blocks))
    return jnp.transpose(out_blocks, (1, 0, 2)).reshape(LENGTH, D)
```

```python
import functools

import jax
import jax.numpy as jnp
import numpy as np
from jax import lax
from jax.experimental import pallas as pl
from jax.experimental.pallas import tpu as pltpu
from jax.sharding import PartitionSpec as P

D = 8192
LANES = 128
SUB = 8
INTERPRET = False


def split(value):
    high = value.astype(jnp.bfloat16)
    return high, (value - high.astype(jnp.float32)).astype(jnp.bfloat16)


def dot(left, right):
    return lax.dot_general(left, right, (((1,), (0,)), ((), ())), preferred_element_type=jnp.float32)


def host_split(value):
    high = value.astype(jnp.bfloat16)
    return high, (value - high.astype(np.float64)).astype(jnp.bfloat16)


@functools.cache
def dft_tables(rows, taps):
    total = rows + taps
    bins = np.arange(total // 2)[:, None]
    points = np.arange(total)[None, :]
    angle = np.pi / total * ((2 * bins + 1) * points % (2 * total))
    table = np.concatenate([np.cos(angle), -np.sin(angle)], 0)
    return (
        host_split(table[:, :taps])
        + host_split(table[:, taps:])
        + host_split(table[:, taps:].T * (2.0 / total))
    )


def from_behind(value, axis):
    count = lax.axis_size(axis)
    return lax.ppermute(value, axis, [(source, source + 1) for source in range(count - 1)])


def spectra_kernel(first, value, taps, head_hi, head_lo, body_hi, body_lo, signal_ref, filter_ref):
    product = (first[...].astype(jnp.float32) * value[...].astype(jnp.float32)).astype(jnp.bfloat16)
    signal_ref[...] = dot(body_hi[...], product) + dot(body_lo[...], product)
    tap_hi, tap_lo = split(taps[...])
    filter_ref[...] = (
        dot(head_hi[...], tap_hi) + dot(head_hi[...], tap_lo) + dot(head_lo[...], tap_hi)
    )


def short_kernel(
    signal, response, halo, gate, head_hi, head_lo, back_hi, back_lo, rate,
    mixed_ref, state_ref, prefix_ref, steps_ref,
):
    rows, width = mixed_ref.shape
    modes = rate.shape[0]
    strip = rows // SUB
    half = signal.shape[0] // 2
    before = halo[...]
    spectrum = signal[...] + dot(head_hi[...], before) + dot(head_lo[...], before)
    sig_re, sig_im = spectrum[:half], spectrum[half:]
    fil_re, fil_im = response[:half], response[half:]
    out_hi, out_lo = split(
        jnp.concatenate([sig_re * fil_re - sig_im * fil_im, sig_re * fil_im + sig_im * fil_re], 0)
    )
    short = dot(back_hi[...], out_hi) + dot(back_hi[...], out_lo) + dot(back_lo[...], out_hi)
    mixed = (gate[...].astype(jnp.float32) * short).astype(jnp.bfloat16)
    mixed_ref[...] = mixed
    place = lax.broadcasted_iota(jnp.int32, (SUB, LANES), 0)
    tiles = width // LANES
    for tile in range(tiles):
        lanes = slice(tile * LANES, (tile + 1) * LANES)
        base = tile * rows
        steps_ref[base : base + rows] = mixed[:, lanes].astype(jnp.float32)
        speed = rate[:, lanes]
        decay = jnp.exp(-speed)
        decays = [jnp.broadcast_to(decay[r : r + 1], (SUB, LANES)) for r in range(modes)]
        first = steps_ref[pl.ds(base, SUB, stride=strip)]
        states = [first] * modes
        for step in range(1, strip):
            drive = steps_ref[pl.ds(base + step, SUB, stride=strip)]
            states = [decays[r] * states[r] + drive for r in range(modes)]
        jump = jnp.exp(-strip * speed)
        for r in range(modes):
            leap = jnp.broadcast_to(jump[r : r + 1], (SUB, LANES))
            total = states[r]
            for hop in (1, 2, 4):
                total = total + leap * jnp.where(place >= hop, pltpu.roll(total, hop, 0), 0.0)
                leap = leap * leap
            row = r * tiles + tile
            state_ref[row : row + 1] = total[SUB - 1 :]
            prefix_ref[row * SUB : (row + 1) * SUB] = jnp.where(
                place >= 1, pltpu.roll(total, 1, 0), 0.0
            )


def scan_kernel(state, speed, span, start_ref):
    count = state.shape[0]
    place = lax.broadcasted_iota(jnp.int32, state.shape, 0)
    leap = jnp.exp(-span * speed[...])
    total = jnp.where(place >= 1, pltpu.roll(state[...], 1, 0), 0.0)
    hop = 1
    while hop < count:
        total = total + leap * jnp.where(place >= hop, pltpu.roll(total, hop, 0), 0.0)
        leap = leap * leap
        hop *= 2
    start_ref[...] = total


def long_kernel(
    mixed, start, prefix, rate, residue, skip, gate, gated_ref, power_ref, steps_ref, long_ref
):
    rows, width = mixed.shape
    modes = rate.shape[0]
    strip = rows // SUB
    place = lax.broadcasted_iota(jnp.int32, (SUB, LANES), 0).astype(jnp.float32)
    tiles = width // LANES
    squares = jnp.zeros((rows, LANES), jnp.float32)
    for tile in range(tiles):
        lanes = slice(tile * LANES, (tile + 1) * LANES)
        base = tile * rows
        steps_ref[base : base + rows] = mixed[:, lanes].astype(jnp.float32)
        speed = rate[:, lanes]
        decay = jnp.exp(-speed)
        weight = residue[:, lanes] * jnp.sqrt(2.0 * speed)
        decays = [jnp.broadcast_to(decay[r : r + 1], (SUB, LANES)) for r in range(modes)]
        weights = [jnp.broadcast_to(weight[r : r + 1], (SUB, LANES)) for r in range(modes)]
        states = []
        for r in range(modes):
            row = r * tiles + tile
            fade = jnp.exp(-strip * place * speed[r : r + 1])
            states.append(prefix[row * SUB : (row + 1) * SUB] + fade * start[row : row + 1])
        for step in range(strip):
            drive = steps_ref[pl.ds(base + step, SUB, stride=strip)]
            states = [decays[r] * states[r] + drive for r in range(modes)]
            sums = [weights[r] * states[r] for r in range(modes)]
            while len(sums) > 1:
                sums = [a + b for a, b in zip(sums[::2], sums[1::2])]
            long_ref[pl.ds(step, SUB, stride=strip)] = sums[0]
        out = (long_ref[...] + skip[:, lanes] * steps_ref[base : base + rows]).astype(jnp.bfloat16)
        gated = gate[:, lanes].astype(jnp.float32) * out.astype(jnp.float32)
        gated_ref[:, lanes] = gated
        squares = squares + gated * gated
    power_ref[...] = lax.dot_general(
        jnp.ones((power_ref.shape[0], LANES), jnp.float32),
        squares,
        (((1,), (1,)), ((), ())),
        precision=lax.Precision.HIGHEST,
        preferred_element_type=jnp.float32,
    )


def call(kernel, outs, *args, scratch=()):
    return pl.pallas_call(
        kernel,
        out_shape=[jax.ShapeDtypeStruct(shape, dtype) for shape, dtype in outs],
        scratch_shapes=[pltpu.VMEM(shape, jnp.float32) for shape in scratch],
        interpret=INTERPRET,
    )(*args)


def on_device(
    first_stream,
    value_stream,
    short_gate,
    out_gate,
    mr_filter,
    li_residue,
    li_rate,
    li_skip,
    norm_gain,
):
    rows, width = first_stream.shape
    taps = mr_filter.shape[0]
    modes = li_rate.shape[0]
    tiles = width // LANES
    head_hi, head_lo, body_hi, body_lo, back_hi, back_lo = map(jnp.asarray, dft_tables(rows, taps))
    tail = (
        first_stream[rows - taps :].astype(jnp.float32)
        * value_stream[rows - taps :].astype(jnp.float32)
    ).astype(jnp.bfloat16)
    before = from_behind(tail, "context")
    f32, bf16 = jnp.float32, jnp.bfloat16
    span = rows + taps
    signal, response = call(
        spectra_kernel,
        [((span, width), f32), ((span, width), f32)],
        first_stream, value_stream, mr_filter, head_hi, head_lo, body_hi, body_lo,
    )
    lots = modes * tiles
    speeds = li_rate.reshape(lots, LANES)
    speed = lax.dynamic_slice_in_dim(speeds, lax.axis_index("context"), 1, 0)
    mixed, state, prefix = call(
        short_kernel,
        [((rows, width), bf16), ((lots, LANES), f32), ((lots * SUB, LANES), f32)],
        signal, response, before, short_gate, head_hi, head_lo, back_hi, back_lo, li_rate,
        scratch=[(tiles * rows, LANES)],
    )
    ends = lax.all_to_all(state, "context", split_axis=0, concat_axis=0, tiled=True)
    starts = call(
        lambda s, v, o: scan_kernel(s, v, float(rows), o), [((lots, LANES), f32)], ends, speed
    )[0]
    start = lax.all_to_all(starts, "context", split_axis=0, concat_axis=0, tiled=True)
    peers = lax.axis_size("channel")
    gated, power = call(
        long_kernel,
        [((rows, width), f32), ((peers, rows), f32)],
        mixed, start, prefix, li_rate, li_residue, li_skip[None], out_gate,
        scratch=[(tiles * rows, LANES), (rows, LANES)],
    )
    powers = lax.all_to_all(power, "channel", split_axis=0, concat_axis=0, tiled=True)
    scale = lax.rsqrt(jnp.sum(powers, axis=0) / D + 1e-06)
    return (gated * scale[:, None] * norm_gain[None, :]).astype(jnp.bfloat16)


def solution(mesh):
    assert mesh.shape["context"] * LANES == 16 * 512
    placed = (
        P("context", "channel"),
        P("context", "channel"),
        P("context", "channel"),
        P("context", "channel"),
        P(None, "channel"),
        P(None, "channel"),
        P(None, "channel"),
        P("channel"),
        P("channel"),
    )
    return jax.shard_map(
        on_device, mesh=mesh, in_specs=placed, out_specs=P("context", "channel"), check_vma=False
    )
```

```python
import functools
import math

import jax
import jax.numpy as jnp
import numpy as np
from jax import lax
from jax.experimental import pallas as pl
from jax.experimental.pallas import tpu as pltpu
from jax.sharding import PartitionSpec as P

D = 8192
LANES = 128
SUB = 8
INTERPRET = False


def split(value):
    high = value.astype(jnp.bfloat16)
    return high, (value - high.astype(jnp.float32)).astype(jnp.bfloat16)


def dot(left, right):
    return lax.dot_general(left, right, (((1,), (0,)), ((), ())), preferred_element_type=jnp.float32)


def host_split(value):
    high = value.astype(jnp.bfloat16)
    return high, (value - high.astype(np.float64)).astype(jnp.bfloat16)


@functools.cache
def dft_tables(rows, taps):
    total = rows + taps
    bins = np.arange(total // 2)[:, None]
    points = np.arange(total)[None, :]
    angle = np.pi / total * ((2 * bins + 1) * points % (2 * total))
    table = np.concatenate([np.cos(angle), -np.sin(angle)], 0)
    return (
        host_split(table[:, :taps])
        + host_split(table[:, taps:])
        + host_split(table[:, taps:].T * (2.0 / total))
    )


def from_behind(value, axis):
    count = lax.axis_size(axis)
    return lax.ppermute(value, axis, [(source, source + 1) for source in range(count - 1)])


def exchange(value, axis, peers, groups):
    rows, width = value.shape
    blocks = value.reshape(peers, rows // peers, width)
    return lax.all_to_all(
        blocks, axis, split_axis=0, concat_axis=0, tiled=True, axis_index_groups=groups
    ).reshape(rows, width)


def spectra_kernel(first, value, taps, head_hi, head_lo, body_hi, body_lo, signal_ref, filter_ref):
    product = (first[...].astype(jnp.float32) * value[...].astype(jnp.float32)).astype(jnp.bfloat16)
    signal_ref[...] = dot(body_hi[...], product) + dot(body_lo[...], product)
    tap_hi, tap_lo = split(taps[...])
    filter_ref[...] = (
        dot(head_hi[...], tap_hi) + dot(head_hi[...], tap_lo) + dot(head_lo[...], tap_hi)
    )


def short_kernel(
    signal, response, halo, gate, head_hi, head_lo, back_hi, back_lo, rate,
    mixed_ref, state_ref, prefix_ref, steps_ref,
):
    rows, width = mixed_ref.shape
    modes = rate.shape[0]
    strip = rows // SUB
    half = signal.shape[0] // 2
    before = halo[...]
    spectrum = signal[...] + dot(head_hi[...], before) + dot(head_lo[...], before)
    sig_re, sig_im = spectrum[:half], spectrum[half:]
    fil_re, fil_im = response[:half], response[half:]
    out_hi, out_lo = split(
        jnp.concatenate([sig_re * fil_re - sig_im * fil_im, sig_re * fil_im + sig_im * fil_re], 0)
    )
    short = dot(back_hi[...], out_hi) + dot(back_hi[...], out_lo) + dot(back_lo[...], out_hi)
    mixed = (gate[...].astype(jnp.float32) * short).astype(jnp.bfloat16)
    mixed_ref[...] = mixed
    place = lax.broadcasted_iota(jnp.int32, (SUB, LANES), 0)
    tiles = width // LANES
    lots = modes * tiles
    for tile in range(tiles):
        lanes = slice(tile * LANES, (tile + 1) * LANES)
        base = tile * rows
        steps_ref[base : base + rows] = mixed[:, lanes].astype(jnp.float32)
        speed = rate[:, lanes]
        decay = jnp.exp(-speed)
        decays = [jnp.broadcast_to(decay[r : r + 1], (SUB, LANES)) for r in range(modes)]
        first = steps_ref[pl.ds(base, SUB, stride=strip)]
        states = [first] * modes
        for step in range(1, strip):
            drive = steps_ref[pl.ds(base + step, SUB, stride=strip)]
            states = [decays[r] * states[r] + drive for r in range(modes)]
        jump = jnp.exp(-strip * speed)
        for r in range(modes):
            leap = jnp.broadcast_to(jump[r : r + 1], (SUB, LANES))
            total = states[r]
            for hop in (1, 2, 4):
                total = total + leap * jnp.where(place >= hop, pltpu.roll(total, hop, 0), 0.0)
                leap = leap * leap
            row = r * tiles + tile
            for peer in range(state_ref.shape[0] // lots):
                state_ref[peer * lots + row : peer * lots + row + 1] = total[SUB - 1 :]
            prefix_ref[row * SUB : (row + 1) * SUB] = jnp.where(
                place >= 1, pltpu.roll(total, 1, 0), 0.0
            )


def chain(parts, position, leap):
    lots = leap.shape[0]
    total = parts[:lots]
    ahead = jnp.zeros_like(total)
    for part in range(1, parts.shape[0] // lots):
        ahead = jnp.where(position == part, total, ahead)
        total = leap * total + parts[part * lots : (part + 1) * lots]
    return ahead, total


def row_kernel(place, states, speeds, ahead_ref, total_ref, *, rows):
    ahead, total = chain(states, place[0], jnp.exp(-rows * speeds[...]))
    ahead_ref[...] = ahead
    lots = ahead.shape[0]
    for peer in range(total_ref.shape[0] // lots):
        total_ref[peer * lots : (peer + 1) * lots] = total


def long_kernel(
    place, mixed, totals, ahead, speeds, prefix, rate, residue, skip, gate,
    gated_ref, power_ref, steps_ref, long_ref,
):
    rows, width = mixed.shape
    side = totals.shape[0] // speeds.shape[0]
    above, _ = chain(totals, place[1], jnp.exp(-float(side * rows) * speeds[...]))
    start = ahead[...] + jnp.exp(-(place[0] * rows).astype(jnp.float32) * speeds[...]) * above
    modes = rate.shape[0]
    strip = rows // SUB
    order = lax.broadcasted_iota(jnp.int32, (SUB, LANES), 0)
    tiles = width // LANES
    squares = jnp.zeros((rows, LANES), jnp.float32)
    for tile in range(tiles):
        lanes = slice(tile * LANES, (tile + 1) * LANES)
        base = tile * rows
        steps_ref[base : base + rows] = mixed[:, lanes].astype(jnp.float32)
        speed = rate[:, lanes]
        decay = jnp.exp(-speed)
        weight = residue[:, lanes] * jnp.sqrt(2.0 * speed)
        decays = [jnp.broadcast_to(decay[r : r + 1], (SUB, LANES)) for r in range(modes)]
        weights = [jnp.broadcast_to(weight[r : r + 1], (SUB, LANES)) for r in range(modes)]
        states = []
        for r in range(modes):
            row = r * tiles + tile
            fade = jnp.exp(-(strip * order).astype(jnp.float32) * speed[r : r + 1])
            states.append(prefix[row * SUB : (row + 1) * SUB] + fade * start[row : row + 1])
        for step in range(strip):
            drive = steps_ref[pl.ds(base + step, SUB, stride=strip)]
            states = [decays[r] * states[r] + drive for r in range(modes)]
            sums = [weights[r] * states[r] for r in range(modes)]
            while len(sums) > 1:
                sums = [a + b for a, b in zip(sums[::2], sums[1::2])]
            long_ref[pl.ds(step, SUB, stride=strip)] = sums[0]
        out = (long_ref[...] + skip[:, lanes] * steps_ref[base : base + rows]).astype(jnp.bfloat16)
        gated = gate[:, lanes].astype(jnp.float32) * out.astype(jnp.float32)
        gated_ref[:, lanes] = gated
        squares = squares + gated * gated
    sums = lax.dot_general(
        jnp.ones((SUB, LANES), jnp.float32),
        squares,
        (((1,), (1,)), ((), ())),
        precision=lax.Precision.HIGHEST,
        preferred_element_type=jnp.float32,
    )
    packed = jnp.zeros((SUB, LANES), jnp.float32)
    for block in range(rows // LANES):
        packed = jnp.where(order == block, sums[:, block * LANES : (block + 1) * LANES], packed)
    for peer in range(power_ref.shape[0] // SUB):
        power_ref[peer * SUB : (peer + 1) * SUB] = packed


def norm_kernel(powers, gated, gain, out_ref, *, channels):
    rows = gated.shape[0]
    total = powers[:SUB]
    for peer in range(1, powers.shape[0] // SUB):
        total = total + powers[peer * SUB : (peer + 1) * SUB]
    scale = lax.rsqrt(total / channels + 1e-06)
    for block in range(rows // LANES):
        column = jnp.broadcast_to(scale[block : block + 1], (LANES, LANES)).T
        tokens = slice(block * LANES, (block + 1) * LANES)
        for tile in range(gated.shape[1] // LANES):
            lanes = slice(tile * LANES, (tile + 1) * LANES)
            out_ref[tokens, lanes] = (gated[tokens, lanes] * column * gain[:, lanes]).astype(
                jnp.bfloat16
            )


def call(kernel, outs, *args, scratch=(), place=None):
    vmem = pl.BlockSpec(memory_space=pltpu.VMEM)
    lead = () if place is None else (place,)
    return pl.pallas_call(
        kernel,
        out_shape=[jax.ShapeDtypeStruct(shape, dtype) for shape, dtype in outs],
        in_specs=[pl.BlockSpec(memory_space=pltpu.SMEM)] * len(lead) + [vmem] * len(args),
        out_specs=[vmem] * len(outs),
        scratch_shapes=[pltpu.VMEM(shape, jnp.float32) for shape in scratch],
        interpret=INTERPRET,
    )(*lead, *args)


def on_device(
    first_stream,
    value_stream,
    short_gate,
    out_gate,
    mr_filter,
    li_residue,
    li_rate,
    li_skip,
    norm_gain,
):
    rows, width = first_stream.shape
    taps = mr_filter.shape[0]
    modes = li_rate.shape[0]
    tiles = width // LANES
    head_hi, head_lo, body_hi, body_lo, back_hi, back_lo = map(jnp.asarray, dft_tables(rows, taps))
    tail = (
        first_stream[rows - taps :].astype(jnp.float32)
        * value_stream[rows - taps :].astype(jnp.float32)
    ).astype(jnp.bfloat16)
    before = from_behind(tail, "context")
    f32, bf16 = jnp.float32, jnp.bfloat16
    span = rows + taps
    signal, response = call(
        spectra_kernel,
        [((span, width), f32), ((span, width), f32)],
        first_stream, value_stream, mr_filter, head_hi, head_lo, body_hi, body_lo,
    )
    lots = modes * tiles
    speeds = li_rate.reshape(lots, LANES)
    shards = lax.axis_size("context")
    side = math.isqrt(shards)
    along_x = [[z * side + x for x in range(side)] for z in range(side)]
    along_z = [[z * side + x for z in range(side)] for x in range(side)]
    shard = lax.axis_index("context")
    place = jnp.stack([shard % side, shard // side])
    mixed, states, prefix = call(
        short_kernel,
        [((rows, width), bf16), ((side * lots, LANES), f32), ((lots * SUB, LANES), f32)],
        signal, response, before, short_gate, head_hi, head_lo, back_hi, back_lo, li_rate,
        scratch=[(tiles * rows, LANES)],
    )
    states = exchange(states, "context", side, along_x)
    ahead, totals = call(
        functools.partial(row_kernel, rows=float(rows)),
        [((lots, LANES), f32), ((side * lots, LANES), f32)],
        states, speeds, place=place,
    )
    totals = exchange(totals, "context", side, along_z)
    peers = lax.axis_size("channel")
    gated, power = call(
        long_kernel,
        [((rows, width), f32), ((peers * SUB, LANES), f32)],
        mixed, totals, ahead, speeds, prefix, li_rate, li_residue, li_skip[None], out_gate,
        scratch=[(tiles * rows, LANES), (rows, LANES)], place=place,
    )
    powers = exchange(power, "channel", peers, None)
    return call(
        functools.partial(norm_kernel, channels=float(D)),
        [((rows, width), bf16)],
        powers, gated, norm_gain[None],
    )[0]


def solution(mesh):
    placed = (
        P("context", "channel"),
        P("context", "channel"),
        P("context", "channel"),
        P("context", "channel"),
        P(None, "channel"),
        P(None, "channel"),
        P(None, "channel"),
        P("channel"),
        P("channel"),
    )
    return jax.shard_map(
        on_device, mesh=mesh, in_specs=placed, out_specs=P("context", "channel"), check_vma=False
    )
```

```python
import functools
import math

import jax
import jax.numpy as jnp
import numpy as np
from jax import lax
from jax.experimental import pallas as pl
from jax.experimental.pallas import tpu as pltpu
from jax.sharding import PartitionSpec as P

D = 8192
LANES = 128
SUB = 8
INTERPRET = False


def split(value):
    high = value.astype(jnp.bfloat16)
    return high, (value - high.astype(jnp.float32)).astype(jnp.bfloat16)


def dot(left, right):
    return lax.dot_general(left, right, (((1,), (0,)), ((), ())), preferred_element_type=jnp.float32)


def host_split(value):
    high = value.astype(jnp.bfloat16)
    return high, (value - high.astype(np.float64)).astype(jnp.bfloat16)


@functools.cache
def dft_tables(rows, taps):
    total = rows + taps
    bins = np.arange(total // 2)[:, None]
    points = np.arange(total)[None, :]
    angle = np.pi / total * ((2 * bins + 1) * points % (2 * total))
    table = np.concatenate([np.cos(angle), -np.sin(angle)], 0)
    return (
        host_split(table[:, :taps])
        + host_split(table[:, taps:])
        + host_split(table[:, taps:].T * (2.0 / total))
    )


def from_behind(value, axis):
    count = lax.axis_size(axis)
    return lax.ppermute(value, axis, [(source, source + 1) for source in range(count - 1)])


def exchange(value, axis, peers, groups):
    rows, width = value.shape
    blocks = value.reshape(peers, rows // peers, width)
    return lax.all_to_all(
        blocks, axis, split_axis=0, concat_axis=0, tiled=True, axis_index_groups=groups
    ).reshape(rows, width)


def end_states(mixed, rate, prefix_ref, end_ref, steps_ref):
    rows, width = mixed.shape
    modes = rate.shape[0]
    strip = rows // SUB
    order = lax.broadcasted_iota(jnp.int32, (SUB, LANES), 0)
    for tile in range(width // LANES):
        lanes = slice(tile * LANES, (tile + 1) * LANES)
        base = tile * rows
        steps_ref[base : base + rows] = mixed[:, lanes].astype(jnp.float32)
        speed = rate[:, lanes]
        decay = jnp.exp(-speed)
        decays = [jnp.broadcast_to(decay[r : r + 1], (SUB, LANES)) for r in range(modes)]
        states = [steps_ref[pl.ds(base, SUB, stride=strip)]] * modes
        for step in range(1, strip):
            drive = steps_ref[pl.ds(base + step, SUB, stride=strip)]
            states = [decays[r] * states[r] + drive for r in range(modes)]
        jump = jnp.exp(-strip * speed)
        for r in range(modes):
            leap = jnp.broadcast_to(jump[r : r + 1], (SUB, LANES))
            total = states[r]
            for hop in (1, 2, 4):
                total = total + leap * jnp.where(order >= hop, pltpu.roll(total, hop, 0), 0.0)
                leap = leap * leap
            row = tile * modes + r
            end_ref[row : row + 1] = total[SUB - 1 :]
            prefix_ref[row * SUB : (row + 1) * SUB] = jnp.where(
                order >= 1, pltpu.roll(total, 1, 0), 0.0
            )


def respond(spectrum, response, back_hi, back_lo):
    half = spectrum.shape[0] // 2
    sig_re, sig_im = spectrum[:half], spectrum[half:]
    fil_re, fil_im = response[:half], response[half:]
    out_hi, out_lo = split(
        jnp.concatenate([sig_re * fil_re - sig_im * fil_im, sig_re * fil_im + sig_im * fil_re], 0)
    )
    return dot(back_hi, out_hi) + dot(back_hi, out_lo) + dot(back_lo, out_hi)


def local_kernel(
    first, value, taps, gate, head_hi, head_lo, body_hi, body_lo, back_hi, back_lo, rate, skip, gain,
    response_ref, short_ref, mixed_ref, prefix_ref, end_ref, rows_ref, steps_ref,
):
    rows_ref[0:1] = skip[...]
    rows_ref[1:2] = gain[...]
    product = (first[...].astype(jnp.float32) * value[...].astype(jnp.float32)).astype(jnp.bfloat16)
    spectrum = dot(body_hi[...], product) + dot(body_lo[...], product)
    tap_hi, tap_lo = split(taps[...])
    response = dot(head_hi[...], tap_hi) + dot(head_hi[...], tap_lo) + dot(head_lo[...], tap_hi)
    response_ref[...] = response
    short = respond(spectrum, response, back_hi[...], back_lo[...])
    half = mixed_ref.shape[0]
    short_ref[...] = short[:half]
    mixed = (gate[half:].astype(jnp.float32) * short[half:]).astype(jnp.bfloat16)
    mixed_ref[...] = mixed
    end_states(mixed, rate, prefix_ref, end_ref, steps_ref)


def halo_kernel(
    response, short, halo, gate, head_hi, head_lo, back_hi, back_lo, rate, last,
    mixed_ref, prefix_ref, end_ref, state_ref, steps_ref,
):
    half = mixed_ref.shape[0]
    before = halo[...]
    spectrum = dot(head_hi[...], before) + dot(head_lo[...], before)
    whole = short[...] + respond(spectrum, response, back_hi[:half], back_lo[:half])
    mixed = (gate[:half].astype(jnp.float32) * whole).astype(jnp.bfloat16)
    mixed_ref[...] = mixed
    end_states(mixed, rate, prefix_ref, end_ref, steps_ref)
    state = jnp.exp(-float(half) * stacked(rate)) * end_ref[...] + last[...]
    lots = state.shape[0]
    for peer in range(state_ref.shape[0] // lots):
        state_ref[peer * lots : (peer + 1) * lots] = state


def stacked(rate):
    value = rate[...]
    return jnp.concatenate(
        [value[:, lane : lane + LANES] for lane in range(0, value.shape[1], LANES)], 0
    )


def chain(parts, position, leap):
    lots = leap.shape[0]
    total = parts[:lots]
    ahead = jnp.zeros_like(total)
    for part in range(1, parts.shape[0] // lots):
        ahead = jnp.where(position == part, total, ahead)
        total = leap * total + parts[part * lots : (part + 1) * lots]
    return ahead, total


def row_kernel(states, rate, ahead_ref, total_ref, *, rows, side):
    position = lax.rem(lax.axis_index("context"), side)
    ahead, total = chain(states, position, jnp.exp(-float(rows) * stacked(rate)))
    ahead_ref[...] = ahead
    lots = ahead.shape[0]
    for peer in range(total_ref.shape[0] // lots):
        total_ref[peer * lots : (peer + 1) * lots] = total


def long_kernel(
    mixed_head, mixed_tail, prefix_head, prefix_tail, end, totals, ahead, rate, residue, per_channel, gate,
    gated_ref, power_ref, steps_ref, long_ref, *, side,
):
    half, width = mixed_head.shape
    rows = 2 * half
    modes = rate.shape[0]
    strip = half // SUB
    shard = lax.axis_index("context")
    speeds = stacked(rate)
    above, _ = chain(totals, lax.div(shard, side), jnp.exp(-float(side * rows) * speeds))
    shift = (lax.rem(shard, side) * rows).astype(jnp.float32)
    start = ahead[...] + jnp.exp(-shift * speeds) * above
    middle = jnp.exp(-float(half) * speeds) * start + end[...]
    order = lax.broadcasted_iota(jnp.int32, (SUB, LANES), 0)
    offset = (strip * order).astype(jnp.float32)
    squares = [jnp.zeros((half, LANES), jnp.float32) for _ in range(2)]
    for tile in range(width // LANES):
        lanes = slice(tile * LANES, (tile + 1) * LANES)
        speed = rate[:, lanes]
        decay = jnp.exp(-speed)
        weight = residue[:, lanes] * jnp.sqrt(2.0 * speed)
        decays = [jnp.broadcast_to(decay[r : r + 1], (SUB, LANES)) for r in range(modes)]
        weights = [jnp.broadcast_to(weight[r : r + 1], (SUB, LANES)) for r in range(modes)]
        fades = [jnp.exp(-offset * speed[r : r + 1]) for r in range(modes)]
        for part, (mixed, prefix, begin) in enumerate(
            ((mixed_head, prefix_head, start), (mixed_tail, prefix_tail, middle))
        ):
            base = (2 * tile + part) * half
            steps_ref[base : base + half] = mixed[:, lanes].astype(jnp.float32)
            states = []
            for r in range(modes):
                row = tile * modes + r
                states.append(
                    prefix[row * SUB : (row + 1) * SUB] + fades[r] * begin[row : row + 1]
                )
            for step in range(strip):
                drive = steps_ref[pl.ds(base + step, SUB, stride=strip)]
                states = [decays[r] * states[r] + drive for r in range(modes)]
                sums = [weights[r] * states[r] for r in range(modes)]
                while len(sums) > 1:
                    sums = [a + b for a, b in zip(sums[::2], sums[1::2])]
                long_ref[pl.ds(base + step, SUB, stride=strip)] = sums[0]
            out = (
                long_ref[base : base + half] + per_channel[0:1, lanes] * steps_ref[base : base + half]
            ).astype(jnp.bfloat16)
            tokens = slice(part * half, (part + 1) * half)
            gated = gate[tokens, lanes].astype(jnp.float32) * out.astype(jnp.float32)
            gated_ref[tokens, lanes] = gated * per_channel[1:2, lanes]
            squares[part] = squares[part] + gated * gated
    packed = jnp.zeros((SUB, LANES), jnp.float32)
    for part in range(2):
        sums = lax.dot_general(
            jnp.ones((SUB, LANES), jnp.float32),
            squares[part],
            (((1,), (1,)), ((), ())),
            precision=lax.Precision.HIGHEST,
            preferred_element_type=jnp.float32,
        )
        packed = jnp.where(order == part, sums, packed)
    for peer in range(power_ref.shape[0] // SUB):
        power_ref[peer * SUB : (peer + 1) * SUB] = packed


def norm_kernel(powers, gated, out_ref, *, channels):
    rows = gated.shape[0]
    total = powers[:SUB]
    for peer in range(1, powers.shape[0] // SUB):
        total = total + powers[peer * SUB : (peer + 1) * SUB]
    scale = lax.rsqrt(total / channels + 1e-06)
    for block in range(rows // LANES):
        column = jnp.broadcast_to(scale[block : block + 1], (LANES, LANES)).T
        tokens = slice(block * LANES, (block + 1) * LANES)
        for tile in range(gated.shape[1] // LANES):
            lanes = slice(tile * LANES, (tile + 1) * LANES)
            out_ref[tokens, lanes] = (gated[tokens, lanes] * column).astype(jnp.bfloat16)


def call(kernel, outs, *args, scratch=()):
    vmem = pl.BlockSpec(memory_space=pltpu.VMEM)
    return pl.pallas_call(
        kernel,
        out_shape=[jax.ShapeDtypeStruct(shape, dtype) for shape, dtype in outs],
        in_specs=[vmem] * len(args),
        out_specs=[vmem] * len(outs),
        scratch_shapes=[pltpu.VMEM(shape, jnp.float32) for shape in scratch],
        compiler_params=pltpu.CompilerParams(vmem_limit_bytes=16 << 20),
        interpret=INTERPRET,
    )(*args)


def on_device(
    first_stream,
    value_stream,
    short_gate,
    out_gate,
    mr_filter,
    li_residue,
    li_rate,
    li_skip,
    norm_gain,
):
    rows, width = first_stream.shape
    taps = mr_filter.shape[0]
    modes = li_rate.shape[0]
    tiles = width // LANES
    head_hi, head_lo, body_hi, body_lo, back_hi, back_lo = map(jnp.asarray, dft_tables(rows, taps))
    tail = (
        first_stream[rows - taps :].astype(jnp.float32)
        * value_stream[rows - taps :].astype(jnp.float32)
    ).astype(jnp.bfloat16)
    before = from_behind(tail, "context")
    f32, bf16 = jnp.float32, jnp.bfloat16
    half = rows // 2
    assert half == taps == LANES
    lots = modes * tiles
    strips = (lots * SUB, LANES)
    response, short, mixed_tail, prefix_tail, last, per_channel = call(
        local_kernel,
        [
            ((rows + taps, width), f32), ((half, width), f32), ((half, width), bf16),
            (strips, f32), ((lots, LANES), f32), ((2, width), f32),
        ],
        first_stream, value_stream, mr_filter, short_gate,
        head_hi, head_lo, body_hi, body_lo, back_hi, back_lo, li_rate, li_skip[None], norm_gain[None],
        scratch=[(tiles * half, LANES)],
    )
    side = math.isqrt(lax.axis_size("context"))
    along_x = [[z * side + x for x in range(side)] for z in range(side)]
    along_z = [[z * side + x for z in range(side)] for x in range(side)]
    mixed_head, prefix_head, end, states = call(
        halo_kernel,
        [
            ((half, width), bf16), (strips, f32), ((lots, LANES), f32),
            ((side * lots, LANES), f32),
        ],
        response, short, before, short_gate, head_hi, head_lo, back_hi, back_lo, li_rate, last,
        scratch=[(tiles * half, LANES)],
    )
    states = exchange(states, "context", side, along_x)
    ahead, totals = call(
        functools.partial(row_kernel, rows=rows, side=side),
        [((lots, LANES), f32), ((side * lots, LANES), f32)],
        states, li_rate,
    )
    totals = exchange(totals, "context", side, along_z)
    peers = lax.axis_size("channel")
    gated, power = call(
        functools.partial(long_kernel, side=side),
        [((rows, width), f32), ((peers * SUB, LANES), f32)],
        mixed_head, mixed_tail, prefix_head, prefix_tail, end, totals, ahead,
        li_rate, li_residue, per_channel, out_gate,
        scratch=[(tiles * rows, LANES), (tiles * rows, LANES)],
    )
    powers = exchange(power, "channel", peers, None)
    return call(
        functools.partial(norm_kernel, channels=float(D)),
        [((rows, width), bf16)],
        powers, gated,
    )[0]


def solution(mesh):
    placed = (
        P("context", "channel"),
        P("context", "channel"),
        P("context", "channel"),
        P("context", "channel"),
        P(None, "channel"),
        P(None, "channel"),
        P(None, "channel"),
        P("channel"),
        P("channel"),
    )
    return jax.shard_map(
        on_device, mesh=mesh, in_specs=placed, out_specs=P("context", "channel"), check_vma=False
    )
```

```python
import functools
import math

import jax
import jax.numpy as jnp
import numpy as np
from jax import lax
from jax.experimental import pallas as pl
from jax.experimental.pallas import tpu as pltpu
from jax.sharding import PartitionSpec as P

D = 8192
LANES = 128
SUB = 8
INTERPRET = False


def split(value):
    high = value.astype(jnp.bfloat16)
    return high, (value - high.astype(jnp.float32)).astype(jnp.bfloat16)


def dot(left, right):
    return lax.dot_general(left, right, (((1,), (0,)), ((), ())), preferred_element_type=jnp.float32)


def host_split(value):
    high = value.astype(jnp.bfloat16)
    return high, (value - high.astype(np.float64)).astype(jnp.bfloat16)


@functools.cache
def dft_tables(rows, taps):
    total = rows + taps
    bins = np.arange(total // 2)[:, None]
    points = np.arange(total)[None, :]
    angle = np.pi / total * ((2 * bins + 1) * points % (2 * total))
    table = np.concatenate([np.cos(angle), -np.sin(angle)], 0)
    return (
        host_split(table[:, :taps])
        + host_split(table[:, taps:])
        + host_split(table[:, taps:].T * (2.0 / total))
    )


def from_behind(value, axis):
    count = lax.axis_size(axis)
    return lax.ppermute(value, axis, [(source, source + 1) for source in range(count - 1)])


def exchange(value, axis, peers, groups):
    rows, width = value.shape
    blocks = value.reshape(peers, rows // peers, width)
    return lax.all_to_all(
        blocks, axis, split_axis=0, concat_axis=0, tiled=True, axis_index_groups=groups
    ).reshape(rows, width)


def end_states(mixed, rate, prefix_ref, end_ref, steps_ref):
    rows, width = mixed.shape
    modes = rate.shape[0]
    strip = rows // SUB
    order = lax.broadcasted_iota(jnp.int32, (SUB, LANES), 0)
    for tile in range(width // LANES):
        lanes = slice(tile * LANES, (tile + 1) * LANES)
        base = tile * rows
        steps_ref[base : base + rows] = mixed[:, lanes].astype(jnp.float32)
        speed = rate[:, lanes]
        decay = jnp.exp(-speed)
        decays = [jnp.broadcast_to(decay[r : r + 1], (SUB, LANES)) for r in range(modes)]
        states = [steps_ref[pl.ds(base, SUB, stride=strip)]] * modes
        for step in range(1, strip):
            drive = steps_ref[pl.ds(base + step, SUB, stride=strip)]
            states = [decays[r] * states[r] + drive for r in range(modes)]
        jump = jnp.exp(-strip * speed)
        for r in range(modes):
            leap = jnp.broadcast_to(jump[r : r + 1], (SUB, LANES))
            total = states[r]
            for hop in (1, 2, 4):
                total = total + leap * jnp.where(order >= hop, pltpu.roll(total, hop, 0), 0.0)
                leap = leap * leap
            row = tile * modes + r
            end_ref[row : row + 1] = total[SUB - 1 :]
            prefix_ref[row * SUB : (row + 1) * SUB] = jnp.where(
                order >= 1, pltpu.roll(total, 1, 0), 0.0
            )


def respond(spectrum, response, back_hi, back_lo):
    half = spectrum.shape[0] // 2
    sig_re, sig_im = spectrum[:half], spectrum[half:]
    fil_re, fil_im = response[:half], response[half:]
    out_hi, out_lo = split(
        jnp.concatenate([sig_re * fil_re - sig_im * fil_im, sig_re * fil_im + sig_im * fil_re], 0)
    )
    return dot(back_hi, out_hi) + dot(back_hi, out_lo) + dot(back_lo, out_hi)


def local_kernel(
    first, value, taps, gate, out_gate, rate, residue, skip, gain,
    head_hi, head_lo, body_hi, body_lo, back_hi, back_lo,
    response_ref, short_ref, mixed_ref, prefix_ref, end_ref,
    gate_ref, out_gate_ref, rate_ref, residue_ref, skip_ref, gain_ref,
    head_hi_ref, head_lo_ref, back_hi_ref, back_lo_ref,
    first_ref, value_ref, taps_ref, body_hi_ref, body_lo_ref, steps_ref, sems,
):
    moves = (
        (first, first_ref), (value, value_ref), (body_hi, body_hi_ref), (body_lo, body_lo_ref),
        (taps, taps_ref), (head_hi, head_hi_ref), (head_lo, head_lo_ref), (back_hi, back_hi_ref),
        (back_lo, back_lo_ref), (gate, gate_ref), (rate, rate_ref), (residue, residue_ref),
        (skip, skip_ref), (gain, gain_ref), (out_gate, out_gate_ref),
    )
    copies = [
        pltpu.make_async_copy(source, target, sems.at[index])
        for index, (source, target) in enumerate(moves)
    ]
    for copy in copies:
        copy.start()
    for copy in copies[:4]:
        copy.wait()
    product = (first_ref[...].astype(jnp.float32) * value_ref[...].astype(jnp.float32)).astype(
        jnp.bfloat16
    )
    spectrum = dot(body_hi_ref[...], product) + dot(body_lo_ref[...], product)
    for copy in copies[4:]:
        copy.wait()
    tap_hi, tap_lo = split(taps_ref[...])
    response = (
        dot(head_hi_ref[...], tap_hi) + dot(head_hi_ref[...], tap_lo) + dot(head_lo_ref[...], tap_hi)
    )
    response_ref[...] = response
    short = respond(spectrum, response, back_hi_ref[...], back_lo_ref[...])
    half = mixed_ref.shape[0]
    short_ref[...] = short[:half]
    mixed = (gate_ref[half:].astype(jnp.float32) * short[half:]).astype(jnp.bfloat16)
    mixed_ref[...] = mixed
    end_states(mixed, rate_ref, prefix_ref, end_ref, steps_ref)


def halo_kernel(
    response, short, halo, gate, head_hi, head_lo, back_hi, back_lo, rate, last,
    mixed_ref, prefix_ref, end_ref, state_ref, steps_ref,
):
    half = mixed_ref.shape[0]
    before = halo[...]
    spectrum = dot(head_hi[...], before) + dot(head_lo[...], before)
    whole = short[...] + respond(spectrum, response, back_hi[:half], back_lo[:half])
    mixed = (gate[:half].astype(jnp.float32) * whole).astype(jnp.bfloat16)
    mixed_ref[...] = mixed
    end_states(mixed, rate, prefix_ref, end_ref, steps_ref)
    state = jnp.exp(-float(half) * stacked(rate)) * end_ref[...] + last[...]
    lots = state.shape[0]
    for peer in range(state_ref.shape[0] // lots):
        state_ref[peer * lots : (peer + 1) * lots] = state


def stacked(rate):
    value = rate[...]
    return jnp.concatenate(
        [value[:, lane : lane + LANES] for lane in range(0, value.shape[1], LANES)], 0
    )


def chain(parts, position, leap):
    lots = leap.shape[0]
    total = parts[:lots]
    ahead = jnp.zeros_like(total)
    for part in range(1, parts.shape[0] // lots):
        ahead = jnp.where(position == part, total, ahead)
        total = leap * total + parts[part * lots : (part + 1) * lots]
    return ahead, total


def row_kernel(states, rate, ahead_ref, total_ref, *, rows, side):
    position = lax.rem(lax.axis_index("context"), side)
    ahead, total = chain(states, position, jnp.exp(-float(rows) * stacked(rate)))
    ahead_ref[...] = ahead
    lots = ahead.shape[0]
    for peer in range(total_ref.shape[0] // lots):
        total_ref[peer * lots : (peer + 1) * lots] = total


def long_kernel(
    mixed_head, mixed_tail, prefix_head, prefix_tail, end, totals, ahead, rate, residue, skip, gain, gate,
    gated_ref, power_ref, steps_ref, long_ref, *, side,
):
    half, width = mixed_head.shape
    rows = 2 * half
    modes = rate.shape[0]
    strip = half // SUB
    shard = lax.axis_index("context")
    speeds = stacked(rate)
    above, _ = chain(totals, lax.div(shard, side), jnp.exp(-float(side * rows) * speeds))
    shift = (lax.rem(shard, side) * rows).astype(jnp.float32)
    start = ahead[...] + jnp.exp(-shift * speeds) * above
    middle = jnp.exp(-float(half) * speeds) * start + end[...]
    order = lax.broadcasted_iota(jnp.int32, (SUB, LANES), 0)
    offset = (strip * order).astype(jnp.float32)
    squares = [jnp.zeros((half, LANES), jnp.float32) for _ in range(2)]
    for tile in range(width // LANES):
        lanes = slice(tile * LANES, (tile + 1) * LANES)
        speed = rate[:, lanes]
        decay = jnp.exp(-speed)
        weight = residue[:, lanes] * jnp.sqrt(2.0 * speed)
        decays = [jnp.broadcast_to(decay[r : r + 1], (SUB, LANES)) for r in range(modes)]
        weights = [jnp.broadcast_to(weight[r : r + 1], (SUB, LANES)) for r in range(modes)]
        fades = [jnp.exp(-offset * speed[r : r + 1]) for r in range(modes)]
        for part, (mixed, prefix, begin) in enumerate(
            ((mixed_head, prefix_head, start), (mixed_tail, prefix_tail, middle))
        ):
            base = (2 * tile + part) * half
            steps_ref[base : base + half] = mixed[:, lanes].astype(jnp.float32)
            states = []
            for r in range(modes):
                row = tile * modes + r
                states.append(
                    prefix[row * SUB : (row + 1) * SUB] + fades[r] * begin[row : row + 1]
                )
            for step in range(strip):
                drive = steps_ref[pl.ds(base + step, SUB, stride=strip)]
                states = [decays[r] * states[r] + drive for r in range(modes)]
                sums = [weights[r] * states[r] for r in range(modes)]
                while len(sums) > 1:
                    sums = [a + b for a, b in zip(sums[::2], sums[1::2])]
                long_ref[pl.ds(base + step, SUB, stride=strip)] = sums[0]
            out = (
                long_ref[base : base + half] + skip[:, lanes] * steps_ref[base : base + half]
            ).astype(jnp.bfloat16)
            tokens = slice(part * half, (part + 1) * half)
            gated = gate[tokens, lanes].astype(jnp.float32) * out.astype(jnp.float32)
            gated_ref[tokens, lanes] = gated * gain[:, lanes]
            squares[part] = squares[part] + gated * gated
    packed = jnp.zeros((SUB, LANES), jnp.float32)
    for part in range(2):
        sums = lax.dot_general(
            jnp.ones((SUB, LANES), jnp.float32),
            squares[part],
            (((1,), (1,)), ((), ())),
            precision=lax.Precision.HIGHEST,
            preferred_element_type=jnp.float32,
        )
        packed = jnp.where(order == part, sums, packed)
    for peer in range(power_ref.shape[0] // SUB):
        power_ref[peer * SUB : (peer + 1) * SUB] = packed


def norm_kernel(powers, gated, out_ref, *, channels):
    rows = gated.shape[0]
    total = powers[:SUB]
    for peer in range(1, powers.shape[0] // SUB):
        total = total + powers[peer * SUB : (peer + 1) * SUB]
    scale = lax.rsqrt(total / channels + 1e-06)
    for block in range(rows // LANES):
        column = jnp.broadcast_to(scale[block : block + 1], (LANES, LANES)).T
        tokens = slice(block * LANES, (block + 1) * LANES)
        for tile in range(gated.shape[1] // LANES):
            lanes = slice(tile * LANES, (tile + 1) * LANES)
            out_ref[tokens, lanes] = (gated[tokens, lanes] * column).astype(jnp.bfloat16)


def call(kernel, outs, *args, scratch=(), fetch=False):
    vmem = pl.BlockSpec(memory_space=pltpu.VMEM)
    if fetch and not INTERPRET:
        args = [pltpu.with_memory_space_constraint(array, pltpu.HBM) for array in args]
    scratches = [pltpu.VMEM(shape, dtype) for shape, dtype in scratch]
    return pl.pallas_call(
        kernel,
        out_shape=[jax.ShapeDtypeStruct(shape, dtype) for shape, dtype in outs],
        in_specs=[pl.BlockSpec(memory_space=pltpu.HBM) if fetch else vmem] * len(args),
        out_specs=[vmem] * len(outs),
        scratch_shapes=scratches + ([pltpu.SemaphoreType.DMA((len(args),))] if fetch else []),
        compiler_params=pltpu.CompilerParams(vmem_limit_bytes=16 << 20),
        interpret=INTERPRET,
    )(*args)


def on_device(
    first_stream,
    value_stream,
    short_gate,
    out_gate,
    mr_filter,
    li_residue,
    li_rate,
    li_skip,
    norm_gain,
):
    rows, width = first_stream.shape
    taps = mr_filter.shape[0]
    modes = li_rate.shape[0]
    tiles = width // LANES
    head_hi, head_lo, body_hi, body_lo, back_hi, back_lo = map(jnp.asarray, dft_tables(rows, taps))
    tail = (
        first_stream[rows - taps :].astype(jnp.float32)
        * value_stream[rows - taps :].astype(jnp.float32)
    ).astype(jnp.bfloat16)
    before = from_behind(tail, "context")
    f32, bf16 = jnp.float32, jnp.bfloat16
    half = rows // 2
    assert half == taps == LANES
    lots = modes * tiles
    strips = (lots * SUB, LANES)
    skip, gain = li_skip[None], norm_gain[None]
    kept = [short_gate, out_gate, li_rate, li_residue, skip, gain]
    kept += [head_hi, head_lo, back_hi, back_lo]
    (
        response, short, mixed_tail, prefix_tail, last,
        gate, last_gate, rate, residue, skip, gain, head_hi, head_lo, back_hi, back_lo,
    ) = call(
        local_kernel,
        [
            ((rows + taps, width), f32), ((half, width), f32), ((half, width), bf16),
            (strips, f32), ((lots, LANES), f32),
        ] + [(array.shape, array.dtype) for array in kept],
        first_stream, value_stream, mr_filter, short_gate, out_gate, li_rate, li_residue, skip, gain,
        head_hi, head_lo, body_hi, body_lo, back_hi, back_lo,
        scratch=[
            (array.shape, array.dtype)
            for array in (first_stream, value_stream, mr_filter, body_hi, body_lo)
        ] + [((tiles * half, LANES), f32)],
        fetch=True,
    )
    side = math.isqrt(lax.axis_size("context"))
    along_x = [[z * side + x for x in range(side)] for z in range(side)]
    along_z = [[z * side + x for z in range(side)] for x in range(side)]
    mixed_head, prefix_head, end, states = call(
        halo_kernel,
        [
            ((half, width), bf16), (strips, f32), ((lots, LANES), f32),
            ((side * lots, LANES), f32),
        ],
        response, short, before, gate, head_hi, head_lo, back_hi, back_lo, rate, last,
        scratch=[((tiles * half, LANES), f32)],
    )
    states = exchange(states, "context", side, along_x)
    ahead, totals = call(
        functools.partial(row_kernel, rows=rows, side=side),
        [((lots, LANES), f32), ((side * lots, LANES), f32)],
        states, rate,
    )
    totals = exchange(totals, "context", side, along_z)
    peers = lax.axis_size("channel")
    gated, power = call(
        functools.partial(long_kernel, side=side),
        [((rows, width), f32), ((peers * SUB, LANES), f32)],
        mixed_head, mixed_tail, prefix_head, prefix_tail, end, totals, ahead,
        rate, residue, skip, gain, last_gate,
        scratch=[((tiles * rows, LANES), f32), ((tiles * rows, LANES), f32)],
    )
    powers = exchange(power, "channel", peers, None)
    return call(
        functools.partial(norm_kernel, channels=float(D)),
        [((rows, width), bf16)],
        powers, gated,
    )[0]


def solution(mesh):
    placed = (
        P("context", "channel"),
        P("context", "channel"),
        P("context", "channel"),
        P("context", "channel"),
        P(None, "channel"),
        P(None, "channel"),
        P(None, "channel"),
        P("channel"),
        P("channel"),
    )
    return jax.shard_map(
        on_device, mesh=mesh, in_specs=placed, out_specs=P("context", "channel"), check_vma=False
    )
```
